32 devices in a mesh: groups: 2 (over x), seq: 16 (over z, y, core).
Axes of the slice: x: 2, y: 2, z: 4, core: 2. Of those that a mesh axis runs over, the one named last changes fastest.
Arguments:
- signal: bfloat16 [32768, 768], P(('groups', 'seq')), parts along dimension 0, may hold values from -6 to 6
- norm_gain: float32 [768], replicated, may hold values from 0.1 to 1.9
- conv_weight: bfloat16 [3, 768, 384], replicated, may hold values from -0.125 to 0.125
- output_weight: bfloat16 [384, 768], replicated, may hold values from -0.3125 to 0.3125
- cotangent: bfloat16 [32768, 768], P(('groups', 'seq')), parts along dimension 0, may hold values from -6 to 6
Outputs:
- block_out: bfloat16 [32768, 768], P(('groups', 'seq')), parts along dimension 0
- signal_grad: bfloat16 [32768, 768], P(('groups', 'seq')), parts along dimension 0
- conv_grad: float32 [6, 768, 384], P('groups'), parts along dimension 0
- output_grad: float32 [768, 768], P('groups'), parts along dimension 0
The draws below stay inside these ranges and needn't reach their ends.
There are 2 independent parts, one for each index of `groups`. The reference program is written for one: setup_inputs(seed, part) draws one part's arguments, and reference() takes and returns one part's arrays. A program takes and returns all parts, laid end to end along the dimension named above; an argument that names none is the same for every part. Nothing has to cross between parts.
All inputs are finite; a program needn't handle non-finite values.
Results may differ from the reference program's by a relative error of at most 0.0056.
Values may be sent and summed in bfloat16 or wider, within the bound.
A program may use at most 128 MiB of HBM per device.

```python
import math
import jax
import jax.numpy as jnp
from jax import lax

STREAM_CHANNELS = 768
H = 384
BINS = 16384


def raised(entries, rng, source, target, parts, factor):
    owner, partner = [(jnp.arange(entries.shape[axis_at]) // (entries.shape[axis_at] // parts)).reshape([-1 if axis == axis_at else 1 for axis in range(entries.ndim)]) for axis_at in (source, target)]
    chosen = jax.random.permutation(rng, parts)[partner]
    strong = (owner == chosen) | (owner == (partner + parts // 2) % parts)
    return jnp.where(strong, factor * entries, entries)


def shard_levels(key, extent, cuts, smallest, top_value):
    def one(position, parts):
        draws = jax.random.uniform(jax.random.fold_in(jax.random.fold_in(key, 6), position), (parts,), jnp.float32, smallest / len(cuts), top_value / len(cuts))
        return jnp.repeat(jnp.exp(draws), extent[position] // parts).reshape((-1,) + (1,) * (len(extent) - position - 1))

    loudness = one(*cuts[0])
    for cut in cuts[1:]:
        loudness = loudness * one(*cut)
    return loudness


def noise(rng, extent, scale, bound, pieces=(), kind=jnp.bfloat16):
    result = jax.random.normal(rng, extent, jnp.float32) * scale
    if len(pieces) > 0:
        result = shard_levels(rng, extent, pieces, -0.22, 0.18) * result
    return jnp.clip(result, min=-bound, max=bound).astype(kind)


def gaussian_with(rng, extent, width, reach, pieces, heavy, held_as=jnp.bfloat16):
    result = width * jax.random.normal(rng, extent, jnp.float32)
    if pieces:
        result = result * shard_levels(rng, extent, pieces, -0.22, 0.18)
    return jnp.clip(raised(result, jax.random.fold_in(rng, 3), *heavy), -reach, reach).astype(held_as)


def setup_inputs(seed: int = 0, part: int = 0) -> dict:
    arg_keys = jax.random.split(jax.random.key(seed), 6)
    part_keys = jax.random.split(jax.random.fold_in(arg_keys[5], part), 6)
    signal = gaussian_with(part_keys[0], (BINS, STREAM_CHANNELS), 1.0, 6.0, ((0, 16),), (0, 1, 16, 2.0))
    norm_gain = jnp.clip(1.0 + 0.18 * jax.random.normal(arg_keys[1], (STREAM_CHANNELS,), jnp.float32), 0.1, 1.9)
    conv_weight = noise(arg_keys[2], (3, STREAM_CHANNELS, H), (3 * STREAM_CHANNELS) ** -0.5, 0.125)
    output_weight = noise(arg_keys[3], (H, STREAM_CHANNELS), H ** -0.5, 0.3125)
    cotangent = gaussian_with(part_keys[4], (BINS, STREAM_CHANNELS), 1.0, 6.0, ((0, 16),), (0, 1, 16, 2.0))
    return {"signal": signal, "norm_gain": norm_gain, "conv_weight": conv_weight, "output_weight": output_weight, "cotangent": cotangent}


epsilon = 1e-06

def gelu_slope(value):
    return 0.5 * (1.0 + jax.scipy.special.erf(value * (1.0 / math.sqrt(2.0)))) + value * jnp.exp(-0.5 * value * value) * (1.0 / math.sqrt(2.0 * math.pi))

def reference(signal, norm_gain, conv_weight, output_weight, cotangent):
    dilation = BINS // 8
    signal_f = signal.astype(jnp.float32)
    mean_square = lax.optimization_barrier(jnp.mean(signal_f * signal_f, axis=-1, keepdims=True))
    inverse_rms = lax.rsqrt(mean_square + epsilon)
    normed = signal_f * inverse_rms * norm_gain
    activated_signal = jax.nn.gelu(normed, approximate=False).astype(jnp.bfloat16)
    empty_rows = jnp.zeros((dilation, STREAM_CHANNELS), jnp.bfloat16)
    earlier_taps = jnp.concatenate([empty_rows, activated_signal[:-dilation]], axis=0)
    later_taps = jnp.concatenate([activated_signal[dilation:], empty_rows], axis=0)
    hidden = jnp.dot(earlier_taps, conv_weight[0], preferred_element_type=jnp.float32)
    hidden = hidden + jnp.dot(activated_signal, conv_weight[1], preferred_element_type=jnp.float32)
    hidden = hidden + jnp.dot(later_taps, conv_weight[2], preferred_element_type=jnp.float32)
    gated = jax.nn.gelu(hidden, approximate=False).astype(jnp.bfloat16)
    block_out = (signal_f + jnp.dot(gated, output_weight, preferred_element_type=jnp.float32)).astype(jnp.bfloat16)
    grad_scale = 1.0 / math.sqrt(BINS)
    gated_grad = jnp.dot(cotangent, output_weight.T, preferred_element_type=jnp.float32)
    hidden_grad = (gated_grad * gelu_slope(hidden)).astype(jnp.bfloat16)
    output_grad = jnp.dot(gated.T, cotangent, preferred_element_type=jnp.float32) * grad_scale
    conv_grad = jnp.stack([jnp.dot(earlier_taps.T, hidden_grad, preferred_element_type=jnp.float32), jnp.dot(activated_signal.T, hidden_grad, preferred_element_type=jnp.float32), jnp.dot(later_taps.T, hidden_grad, preferred_element_type=jnp.float32)]) * grad_scale
    leading_tap = jnp.dot(hidden_grad, conv_weight[0].T, preferred_element_type=jnp.float32)
    trailing_tap = jnp.dot(hidden_grad, conv_weight[2].T, preferred_element_type=jnp.float32)
    float_zero_value = jnp.zeros((dilation, STREAM_CHANNELS), jnp.float32)
    input_gradient = jnp.dot(hidden_grad, conv_weight[1].T, preferred_element_type=jnp.float32)
    input_gradient = input_gradient + jnp.concatenate([leading_tap[dilation:], float_zero_value], axis=0)
    input_gradient = input_gradient + jnp.concatenate([float_zero_value, trailing_tap[:-dilation]], axis=0)
    weighted = input_gradient * gelu_slope(normed) * norm_gain
    inner = lax.optimization_barrier(jnp.mean(weighted * signal_f, axis=-1, keepdims=True))
    cubed = inverse_rms * inverse_rms * inverse_rms
    signal_grad = cotangent.astype(jnp.float32) + weighted * inverse_rms - signal_f * cubed * inner
    return (block_out, signal_grad.astype(jnp.bfloat16), conv_grad, output_grad)
```

```python
import functools
import math

import jax
import jax.numpy as jnp
from jax import lax
from jax.experimental import pallas as pl
from jax.experimental.pallas import tpu as pltpu
from jax.sharding import PartitionSpec as P

epsilon = 1e-06


def passed_along(block, axis, distance):
    devices = range(lax.axis_size(axis))
    route = [(i - distance, i) for i in devices if i - distance in devices]
    return lax.ppermute(block, axis, route)


def gelu_cdf(value):
    return 0.5 * (1.0 + jax.scipy.special.erf(value * (1.0 / math.sqrt(2.0))))


def gelu_slope(value, cdf):
    return cdf + value * jnp.exp(-0.5 * value * value) * (1.0 / math.sqrt(2.0 * math.pi))


def dot(left, right, contract):
    return lax.dot_general(left, right, (contract, ((), ())), preferred_element_type=jnp.float32)


def whole_block(
    devices, signal_hbm, cotangent_hbm, conv_hbm, output_hbm, gain_hbm,
    block_out, signal_grad, grads,
    signal, cotangent, conv_weight, output_weight, norm_gain,
    activated, transposed, cotangent_t, hidden, gated_grad, near_term, gated,
    far_out, far_in, near_out, near_in, hidden_grad, near_grad, far_grad,
    own, give, from_sibling, y_send, from_y, z_send, pieces,
    load_sems,
    far_sems, near_sems, across_sems, relay_sems,
    pair_sems, y_sems, z_sems, zg_sems, yg_sems, back_sems,
):
    channels, width = conv_weight.shape[1:]
    bins = signal.shape[0]
    bf16, f32 = jnp.bfloat16, jnp.float32
    me = lax.axis_index("seq")
    core, odd, depth = me % 2, (me // 2) % 2, me // 4
    levels = devices // 4
    sibling = {"seq": me + 1 - 2 * core}
    partner = {"seq": me + 2 - 4 * odd}
    far_tap, near_tap = 2 - 2 * odd, 2 * odd
    step_sign = 2 * odd - 1
    far_level, back_level = depth + step_sign, depth - step_sign
    has_far = jnp.logical_and(far_level >= 0, far_level < levels)
    has_back = jnp.logical_and(back_level >= 0, back_level < levels)
    far_device = {"seq": lax.rem(me + 4 * step_sign + devices, devices)}
    back_device = {"seq": lax.rem(me - 4 * step_sign + devices, devices)}
    chunk, tile, block = 128, 256, 128
    chunks = bins // chunk
    blocks = width // block
    splits = bins // tile
    half = channels // 2
    piece = half // levels

    def rows(step, size=chunk):
        if isinstance(step, int):
            return pl.ds(step * size, size)
        return pl.ds(pl.multiple_of(step * size, size), size)

    def level(distance):
        other = lax.rem(depth + distance, levels)
        return other, {"seq": other * 4 + odd * 2 + core}

    barrier = pltpu.get_barrier_semaphore()
    pl.semaphore_signal(barrier, inc=1, device_id=sibling)
    pl.semaphore_signal(barrier, inc=1, device_id=partner)
    for distance in range(1, levels):
        pl.semaphore_signal(barrier, inc=1, device_id=level(distance)[1])

    def load_signal(step):
        at = rows(step)
        return pltpu.make_async_copy(signal_hbm.at[at], signal.at[at], load_sems.at[step])

    def load_cotangent(step):
        at = rows(step)
        return pltpu.make_async_copy(
            cotangent_hbm.at[at], cotangent.at[at], load_sems.at[chunks + step]
        )

    conv_load = pltpu.make_async_copy(conv_hbm, conv_weight, load_sems.at[2 * chunks])
    output_load = pltpu.make_async_copy(output_hbm, output_weight, load_sems.at[2 * chunks + 1])
    gain_load = pltpu.make_async_copy(gain_hbm, norm_gain, load_sems.at[2 * chunks + 2])
    gain_load.start()
    load_signal(0).start()
    conv_load.start()
    output_load.start()
    load_cotangent(0).start()

    @pl.loop(1, chunks)
    def _(step):
        load_signal(step).start()
        load_cotangent(step).start()

    @pl.when(jnp.logical_not(has_back))
    def _():
        far_in[...] = jnp.zeros_like(far_in)

    @pl.when(jnp.logical_not(has_far))
    def _():
        far_grad[...] = jnp.zeros_like(far_grad)

    def far_copy(step):
        at = rows(step)
        return pltpu.make_async_remote_copy(
            far_out.at[at], far_in.at[at], far_sems.at[0, step], far_sems.at[1, step],
            device_id=far_device,
        )

    def near_copy(step):
        at = rows(step)
        return pltpu.make_async_remote_copy(
            near_out.at[at], near_in.at[at], near_sems.at[0, step], near_sems.at[1, step],
            device_id=partner,
        )

    def across_copy(column, split):
        at = rows(split, tile)
        return pltpu.make_async_remote_copy(
            hidden_grad.at[column, at], near_grad.at[column, at],
            across_sems.at[0, column, split], across_sems.at[1, column, split],
            device_id=partner,
        )

    def relay_copy(column, split):
        at = rows(split, tile)
        return pltpu.make_async_remote_copy(
            near_grad.at[column, at], far_grad.at[column, at],
            relay_sems.at[0, column, split], relay_sems.at[1, column, split],
            device_id=back_device,
        )

    def gain():
        return norm_gain[...].reshape(1, channels)

    def normalized(at):
        signal_f = signal[at, :].astype(f32)
        mean_square = jnp.mean(signal_f * signal_f, axis=-1, keepdims=True)
        inverse_rms = lax.rsqrt(mean_square + epsilon)
        return signal_f, inverse_rms, signal_f * inverse_rms * gain()

    def activate(step):
        load_signal(step).wait()
        at = rows(step)
        _, _, normed = normalized(at)
        activated[at, :] = (normed * gelu_cdf(normed)).astype(bf16)

    def multiply(step):
        at = rows(step)
        value = activated[at, :]
        far_out[at, :] = dot(value, conv_weight[far_tap], ((1,), (0,))).astype(bf16)
        pl.when(has_far)(far_copy(step).start)
        near_term[at, :] = dot(value, conv_weight[near_tap], ((1,), (0,)))
        hidden[at, :] = dot(value, conv_weight[1], ((1,), (0,)))
        gated_grad[at, :] = dot(cotangent[at, :], output_weight[...], ((1,), (1,)))
        transposed[:, at] = value.T
        cotangent_t[:, at] = cotangent[at, :].T

    def pass_near(step):
        at = rows(step)
        pl.when(has_back)(far_copy(step).wait_recv)
        near_out[at, :] = (near_term[at, :] + far_in[at, :].astype(f32)).astype(bf16)
        near_copy(step).start()

    def finish_hidden(step):
        at = rows(step)
        near_copy(step).wait_recv()
        value = hidden[at, :] + near_in[at, :].astype(f32)
        cdf = gelu_cdf(value)
        result = (gated_grad[at, :] * gelu_slope(value, cdf)).astype(bf16)
        for column in range(blocks):
            hidden_grad[column, at, :] = result[:, column * block : (column + 1) * block]
        gated[at, :] = (value * cdf).astype(bf16)

        @pl.when(lax.rem(step, 2) == 1)
        def _():
            across_copy(0, lax.div(step, 2)).start()

    gain_load.wait()
    activate(0)
    conv_load.wait()
    output_load.wait()
    pl.semaphore_wait(barrier, levels + 1)

    @pl.loop(0, chunks)
    def _(step):
        load_cotangent(step).wait()

        @pl.when(step + 1 < chunks)
        def _():
            activate(step + 1)

        multiply(step)

        @pl.when(step >= 2)
        def _():
            pass_near(step - 2)

        @pl.when(step >= 4)
        def _():
            finish_hidden(step - 4)

    @pl.loop(chunks, chunks + 4)
    def _(step):
        @pl.when(step < chunks + 2)
        def _():
            pass_near(step - 2)

        finish_hidden(step - 4)

    sent = []

    def contribute_first(unit):
        column = unit
        side = slice(column * block, (column + 1) * block)

        @pl.loop(0, channels // tile)
        def _(step):
            at = rows(step, tile)
            output_part = dot(cotangent_t[at, :], gated[:, side], ((1,), (0,)))
            middle_part = dot(transposed[at, :], hidden_grad[column], ((1,), (0,)))
            own[unit, at, :] = jnp.where(core == 0, output_part, middle_part)
            give[unit, at, :] = jnp.where(core == 0, middle_part, output_part).astype(bf16)

        start_pair(unit)

    def contribute_second(unit):
        column = unit - blocks
        for split in range(splits):
            pl.when(has_far)(relay_copy(column, split).wait_recv)

        @pl.loop(0, channels // tile)
        def _(step):
            at = rows(step, tile)
            near_part = dot(transposed[at, :], near_grad[column], ((1,), (0,)))
            far_part = dot(transposed[at, :], far_grad[column], ((1,), (0,)))
            own[unit, at, :] = jnp.where(core == odd, near_part, far_part)
            give[unit, at, :] = jnp.where(core == odd, far_part, near_part).astype(bf16)

        start_pair(unit)

    def pair_copy(unit):
        return pltpu.make_async_remote_copy(
            give.at[unit], from_sibling.at[unit], pair_sems.at[0, unit], pair_sems.at[1, unit],
            device_id=sibling,
        )

    def start_pair(unit):
        copy = pair_copy(unit)
        copy.start()
        sent.append(copy)

    mine = pl.ds(pl.multiple_of(odd * half, half), half)
    theirs = pl.ds(pl.multiple_of((1 - odd) * half, half), half)
    my_piece = pl.ds(pl.multiple_of(odd * half + depth * piece, piece), piece)

    def y_copy(unit):
        return pltpu.make_async_remote_copy(
            y_send.at[unit], from_y.at[unit], y_sems.at[0, unit], y_sems.at[1, unit],
            device_id=partner,
        )

    def z_copy(unit, distance):
        other, device = level(distance)
        return pltpu.make_async_remote_copy(
            z_send.at[unit, pl.ds(pl.multiple_of(other * piece, piece), piece)],
            pieces.at[unit, distance - 1],
            z_sems.at[0, unit, distance - 1], z_sems.at[1, unit, distance - 1],
            device_id=device,
        )

    def landing(unit):
        return grads.at[unit // blocks, core, unit % blocks]

    def zg_copy(unit, distance):
        place = landing(unit).at[my_piece]
        return pltpu.make_async_remote_copy(
            place, place, zg_sems.at[0, unit, distance - 1], zg_sems.at[1, unit, distance - 1],
            device_id=level(distance)[1],
        )

    def yg_copy(unit):
        place = landing(unit).at[mine]
        return pltpu.make_async_remote_copy(
            place, place, yg_sems.at[0, unit], yg_sems.at[1, unit], device_id=partner,
        )

    def back_copy(unit, which):
        place = landing(unit).at[mine if which == 0 else theirs]
        return pltpu.make_async_remote_copy(
            place, place, back_sems.at[0, unit, which], back_sems.at[1, unit, which],
            device_id=sibling,
        )

    def to_y(unit):
        pair_copy(unit).wait_recv()
        y_send[unit] = (
            own[unit, theirs, :] + from_sibling[unit, theirs, :].astype(f32)
        ).astype(bf16)
        copy = y_copy(unit)
        copy.start()
        sent.append(copy)

    def to_z(unit):
        y_copy(unit).wait_recv()
        total = (
            own[unit, mine, :]
            + from_sibling[unit, mine, :].astype(f32)
            + from_y[unit].astype(f32)
        )
        own[unit, mine, :] = total
        z_send[unit] = total.astype(bf16)
        for distance in range(1, levels):
            copy = z_copy(unit, distance)
            copy.start()
            sent.append(copy)

    def from_z(unit):
        for distance in range(1, levels):
            z_copy(unit, distance).wait_recv()
        total = own[unit, my_piece, :]
        for distance in range(1, levels):
            total = total + pieces[unit, distance - 1].astype(f32)
        grads[unit // blocks, core, unit % blocks, my_piece, :] = total.astype(bf16)
        for distance in range(1, levels):
            copy = zg_copy(unit, distance)
            copy.start()
            sent.append(copy)

    def gather_y(unit):
        for distance in range(1, levels):
            zg_copy(unit, distance).wait_recv()
        for copy in (yg_copy(unit), back_copy(unit, 0)):
            copy.start()
            sent.append(copy)

    def gather_back(unit):
        yg_copy(unit).wait_recv()
        copy = back_copy(unit, 1)
        copy.start()
        sent.append(copy)

    def finish(unit):
        back_copy(unit, 0).wait_recv()
        back_copy(unit, 1).wait_recv()

    def relay(item, ahead=splits):
        column, split = divmod(item, splits)
        across_copy(column, split).wait_recv()
        pl.when(has_back)(relay_copy(column, split).start)
        later = item + ahead
        if later < blocks * splits:
            across_copy(*divmod(later, splits)).start()

    def write_out(step):
        at = rows(step, tile)
        block_out[at, :] = (
            signal[at, :].astype(f32) + dot(gated[at, :], output_weight[...], ((1,), (0,)))
        ).astype(bf16)

    def write_grad(step):
        at = rows(step)

        def joined(ref):
            return jnp.concatenate([ref[column, at, :] for column in range(blocks)], axis=1)

        signal_f, inverse_rms, normed = normalized(at)
        input_gradient = (
            dot(joined(hidden_grad), conv_weight[1], ((1,), (1,)))
            + dot(joined(near_grad), conv_weight[near_tap], ((1,), (1,)))
            + dot(joined(far_grad), conv_weight[far_tap], ((1,), (1,)))
        )
        weighted = input_gradient * gelu_slope(normed, gelu_cdf(normed)) * gain()
        inner = jnp.mean(weighted * signal_f, axis=-1, keepdims=True)
        cubed = inverse_rms * inverse_rms * inverse_rms
        signal_grad[at, :] = (
            cotangent[at, :].astype(f32) + weighted * inverse_rms - signal_f * cubed * inner
        ).astype(bf16)

    def write_grads(first, last):
        @pl.loop(first, last)
        def _(step):
            write_grad(step)

    contribute_first(0)
    relay(0)
    relay(1)
    contribute_first(1)
    to_y(0)
    relay(2)
    contribute_first(2)
    to_y(1)
    relay(3)
    write_out(0)
    relay(4)
    to_y(2)
    write_out(1)
    relay(5)
    to_z(0)
    write_out(2)
    relay(6)
    write_out(3)
    contribute_second(3)
    relay(7)
    to_z(1)
    to_y(3)
    relay(8)
    from_z(0)
    to_z(2)
    relay(9)
    contribute_second(4)
    from_z(1)
    relay(10)
    to_y(4)
    to_z(3)
    relay(11)
    gather_y(0)
    from_z(2)
    contribute_second(5)
    gather_y(1)
    from_z(3)
    to_z(4)
    to_y(5)
    gather_back(0)
    gather_y(2)
    write_grads(0, 2)
    from_z(4)
    to_z(5)
    gather_y(3)
    gather_back(1)
    finish(0)
    write_grads(2, 4)
    from_z(5)
    gather_back(2)
    gather_y(4)
    finish(1)
    write_grads(4, 6)
    gather_back(3)
    gather_y(5)
    finish(2)
    write_grads(6, 8)
    gather_back(4)
    finish(3)
    gather_back(5)
    finish(4)
    finish(5)

    for copy in sent:
        copy.wait_send()

    @pl.loop(0, chunks)
    def _(step):
        near_copy(step).wait_send()
        pl.when(has_far)(far_copy(step).wait_send)

    for column in range(blocks):
        for split in range(splits):
            across_copy(column, split).wait_send()
            pl.when(has_back)(relay_copy(column, split).wait_send)


def copy_results(
    grad_scale, block_out, signal_grad, grads, out0, out1, out2, out3, conv_grad, output_grad, sems
):
    blocks = grads.shape[2]
    block = grads.shape[4]
    copies = [
        pltpu.make_async_copy(block_out, out0, sems.at[0]),
        pltpu.make_async_copy(signal_grad, out1, sems.at[1]),
    ]
    for copy in copies:
        copy.start()
    for tap, (batch, owner) in enumerate(((1, 0), (0, 1), (1, 1))):
        for column in range(blocks):
            side = slice(column * block, (column + 1) * block)
            conv_grad[tap, :, side] = grads[batch, owner, column].astype(jnp.float32) * grad_scale
        copies.append(pltpu.make_async_copy(conv_grad.at[tap], out2.at[tap], sems.at[2 + tap]))
        copies[-1].start()
    for column in range(blocks):
        side = slice(column * block, (column + 1) * block)
        output_grad[side, :] = grads[0, 0, column].astype(jnp.float32).T * grad_scale
    copies.append(pltpu.make_async_copy(output_grad, out3, sems.at[5]))
    copies[-1].start()
    for copy in copies:
        copy.wait()


def run_whole_block(signal, norm_gain, conv_weight, output_weight, cotangent):
    devices = lax.axis_size("seq")
    levels = devices // 4
    bins, channels = signal.shape
    width = output_weight.shape[0]
    chunks = bins // 128
    blocks, block, splits = width // 128, 128, bins // 256
    units = 2 * blocks
    bf16, f32 = jnp.bfloat16, jnp.float32
    vmem = pl.BlockSpec(memory_space=pltpu.VMEM)
    hbm = pl.BlockSpec(memory_space=pltpu.HBM)
    dma = pltpu.SemaphoreType.DMA
    narrow = pltpu.VMEM((bins, width), bf16)
    wide = pltpu.VMEM((bins, width), f32)
    stacked = pltpu.VMEM((blocks, bins, block), bf16)
    results = (
        jax.ShapeDtypeStruct((bins, channels), bf16),
        jax.ShapeDtypeStruct((bins, channels), bf16),
        jax.ShapeDtypeStruct((3, channels, width), f32),
        jax.ShapeDtypeStruct((width, channels), f32),
    )
    outs = pl.pallas_call(
        functools.partial(whole_block, devices),
        out_shape=(
            pltpu.VMEM((bins, channels), bf16),
            pltpu.VMEM((bins, channels), bf16),
            pltpu.VMEM((2, 2, blocks, channels, block), bf16),
        ),
        in_specs=[hbm] * 5,
        out_specs=(vmem,) * 3,
        scratch_shapes=[
            pltpu.VMEM((bins, channels), bf16),
            pltpu.VMEM((bins, channels), bf16),
            pltpu.VMEM((3, channels, width), bf16),
            pltpu.VMEM((width, channels), bf16),
            pltpu.VMEM((channels,), f32),
            pltpu.VMEM((bins, channels), bf16),
            pltpu.VMEM((channels, bins), bf16),
            pltpu.VMEM((channels, bins), bf16),
            wide, wide, wide, narrow,
            narrow, narrow, narrow, narrow,
            stacked, stacked, stacked,
            pltpu.VMEM((units, channels, block), f32),
            pltpu.VMEM((units, channels, block), bf16),
            pltpu.VMEM((units, channels, block), bf16),
            pltpu.VMEM((units, channels // 2, block), bf16),
            pltpu.VMEM((units, channels // 2, block), bf16),
            pltpu.VMEM((units, channels // 2, block), bf16),
            pltpu.VMEM((units, levels - 1, channels // 2 // levels, block), bf16),
            dma((2 * chunks + 3,)),
            dma((2, chunks)),
            dma((2, chunks)),
            dma((2, blocks, splits)),
            dma((2, blocks, splits)),
            dma((2, units)),
            dma((2, units)),
            dma((2, units, levels - 1)),
            dma((2, units, levels - 1)),
            dma((2, units)),
            dma((2, units, 2)),
        ],
        compiler_params=pltpu.CompilerParams(
            collective_id=0, has_side_effects=True, vmem_limit_bytes=42 << 20
        ),
        name="whole_block",
    )(*[
        pltpu.with_memory_space_constraint(value, pltpu.HBM)
        for value in (signal, cotangent, conv_weight, output_weight, norm_gain)
    ])
    return pl.pallas_call(
        functools.partial(copy_results, 1.0 / math.sqrt(bins * devices)),
        out_shape=results,
        in_specs=[vmem] * 3,
        out_specs=(hbm,) * 4,
        scratch_shapes=[
            pltpu.VMEM((3, channels, width), f32), pltpu.VMEM((width, channels), f32), dma((6,))
        ],
        compiler_params=pltpu.CompilerParams(vmem_limit_bytes=16 << 20),
        name="copy_results",
    )(*outs)


def shards(signal, norm_gain, conv_weight, output_weight, cotangent):
    devices = lax.axis_size("seq")
    stride = devices // 8
    local_bins = signal.shape[0]
    if devices == 16:
        return run_whole_block(signal, norm_gain, conv_weight, output_weight, cotangent)
    odd = (lax.axis_index("seq") // stride) % 2 == 1
    far_weight = jnp.where(odd, conv_weight[0], conv_weight[2])
    near_weight = jnp.where(odd, conv_weight[2], conv_weight[0])
    far_route, near_route = [], []
    for i in range(devices):
        is_odd = (i // stride) % 2 == 1
        target = i + 2 * stride if is_odd else i - 2 * stride
        if 0 <= target < devices:
            far_route.append((i, target))
        near_route.append((i, i - stride if is_odd else i + stride))

    signal_f = signal.astype(jnp.float32)
    mean_square = jnp.mean(signal_f * signal_f, axis=-1, keepdims=True)
    inverse_rms = lax.rsqrt(mean_square + epsilon)
    normed = signal_f * inverse_rms * norm_gain
    normed_cdf = gelu_cdf(normed)
    activated = (normed * normed_cdf).astype(jnp.bfloat16)

    chunks = 2
    rows = local_bins // chunks
    parts = []
    for j in range(chunks):
        block = activated[j * rows : (j + 1) * rows]
        far = dot(block, far_weight, ((1,), (0,))).astype(jnp.bfloat16)
        parts.append(lax.ppermute(far, "seq", far_route))
    arrived = []
    for j in range(chunks):
        block = activated[j * rows : (j + 1) * rows]
        near = dot(block, near_weight, ((1,), (0,))) + parts[j].astype(jnp.float32)
        arrived.append(lax.ppermute(near.astype(jnp.bfloat16), "seq", near_route))
    hidden = dot(activated, conv_weight[1], ((1,), (0,))) + jnp.concatenate(arrived).astype(
        jnp.float32
    )
    hidden_cdf = gelu_cdf(hidden)
    gated = (hidden * hidden_cdf).astype(jnp.bfloat16)
    gated_grad = dot(cotangent, output_weight, ((1,), (1,)))
    hidden_grad = (gated_grad * gelu_slope(hidden, hidden_cdf)).astype(jnp.bfloat16)
    earlier = passed_along(hidden_grad, "seq", stride)
    later = passed_along(hidden_grad, "seq", -stride)

    grad_scale = 1.0 / math.sqrt(local_bins * devices)
    block_out = (signal_f + dot(gated, output_weight, ((1,), (0,)))).astype(jnp.bfloat16)
    output_term = dot(gated, cotangent, ((0,), (0,))) * grad_scale
    middle_term = dot(activated, hidden_grad, ((0,), (0,))) * grad_scale
    output_grad, middle_grad = lax.psum((output_term, middle_term), "seq")
    first_term = dot(activated, later, ((0,), (0,))) * grad_scale
    last_term = dot(activated, earlier, ((0,), (0,))) * grad_scale
    first_grad, last_grad = lax.psum((first_term, last_term), "seq")
    conv_grad = jnp.stack([first_grad, middle_grad, last_grad])

    input_gradient = (
        dot(hidden_grad, conv_weight[1], ((1,), (1,)))
        + dot(later, conv_weight[0], ((1,), (1,)))
        + dot(earlier, conv_weight[2], ((1,), (1,)))
    )
    weighted = input_gradient * gelu_slope(normed, normed_cdf) * norm_gain
    inner = jnp.mean(weighted * signal_f, axis=-1, keepdims=True)
    cubed = inverse_rms * inverse_rms * inverse_rms
    signal_grad = cotangent.astype(jnp.float32) + weighted * inverse_rms - signal_f * cubed * inner
    return (block_out, signal_grad.astype(jnp.bfloat16), conv_grad, output_grad)


def solution(mesh):
    placed = (P(("groups", "seq"), None), P(), P(), P(), P(("groups", "seq"), None))
    return jax.shard_map(
        shards,
        mesh=mesh,
        in_specs=placed,
        out_specs=(
            P(("groups", "seq"), None),
            P(("groups", "seq"), None),
            P("groups", None, None),
            P("groups", None),
        ),
        check_vma=False,
    )
```

```python
import functools
import math

import jax
import jax.numpy as jnp
from jax import lax
from jax.experimental import pallas as pl
from jax.experimental.pallas import tpu as pltpu
from jax.sharding import PartitionSpec as P

epsilon = 1e-06


def passed_along(block, axis, distance):
    devices = range(lax.axis_size(axis))
    route = [(i - distance, i) for i in devices if i - distance in devices]
    return lax.ppermute(block, axis, route)


def gelu_cdf(value):
    return 0.5 * (1.0 + jax.scipy.special.erf(value * (1.0 / math.sqrt(2.0))))


def gelu_slope(value, cdf):
    return cdf + value * jnp.exp(-0.5 * value * value) * (1.0 / math.sqrt(2.0 * math.pi))


def dot(left, right, contract):
    return lax.dot_general(left, right, (contract, ((), ())), preferred_element_type=jnp.float32)


def whole_block(
    devices, split_last, signal_hbm, cotangent_hbm, conv_hbm, output_hbm, gain_hbm,
    block_out, signal_grad, grads,
    signal, cotangent, conv_weight, output_weight, norm_gain,
    activated, transposed, cotangent_t, hidden, gated_grad, near_term, gated,
    far_out, far_in, near_out, near_in, hidden_grad, near_grad, far_grad,
    own, give, from_sibling, y_send, from_y, z_send, pieces,
    deep_send, deep_pieces, thin_send, from_thin,
    load_sems,
    far_sems, near_sems, across_sems, relay_sems,
    pair_sems, y_sems, z_sems, zg_sems, yg_sems, back_sems,
):
    channels, width = conv_weight.shape[1:]
    bins = signal.shape[0]
    bf16, f32 = jnp.bfloat16, jnp.float32
    me = lax.axis_index("seq")
    core, odd, depth = me % 2, (me // 2) % 2, me // 4
    levels = devices // 4
    sibling = {"seq": me + 1 - 2 * core}
    partner = {"seq": me + 2 - 4 * odd}
    far_tap, near_tap = 2 - 2 * odd, 2 * odd
    step_sign = 2 * odd - 1
    far_level, back_level = depth + step_sign, depth - step_sign
    has_far = jnp.logical_and(far_level >= 0, far_level < levels)
    has_back = jnp.logical_and(back_level >= 0, back_level < levels)
    far_device = {"seq": lax.rem(me + 4 * step_sign + devices, devices)}
    back_device = {"seq": lax.rem(me - 4 * step_sign + devices, devices)}
    chunk, tile, block = 256, 256, 128
    chunks = bins // chunk
    blocks = width // block
    splits = bins // tile
    half = channels // 2
    piece = half // levels
    layer = channels // levels

    def rows(step, size=chunk):
        if isinstance(step, int):
            return pl.ds(step * size, size)
        return pl.ds(pl.multiple_of(step * size, size), size)

    def level(distance):
        other = lax.rem(depth + distance, levels)
        return other, {"seq": other * 4 + odd * 2 + core}

    barrier = pltpu.get_barrier_semaphore()
    pl.semaphore_signal(barrier, inc=1, device_id=sibling)
    pl.semaphore_signal(barrier, inc=1, device_id=partner)
    for distance in range(1, levels):
        pl.semaphore_signal(barrier, inc=1, device_id=level(distance)[1])

    def load_signal(step):
        at = rows(step)
        return pltpu.make_async_copy(signal_hbm.at[at], signal.at[at], load_sems.at[step])

    def load_cotangent(step):
        at = rows(step)
        return pltpu.make_async_copy(
            cotangent_hbm.at[at], cotangent.at[at], load_sems.at[chunks + step]
        )

    conv_load = pltpu.make_async_copy(conv_hbm, conv_weight, load_sems.at[2 * chunks])
    output_load = pltpu.make_async_copy(output_hbm, output_weight, load_sems.at[2 * chunks + 1])
    gain_load = pltpu.make_async_copy(gain_hbm, norm_gain, load_sems.at[2 * chunks + 2])
    gain_load.start()
    load_signal(0).start()
    conv_load.start()
    output_load.start()
    load_cotangent(0).start()

    @pl.loop(1, chunks)
    def _(step):
        load_signal(step).start()
        load_cotangent(step).start()

    @pl.when(jnp.logical_not(has_back))
    def _():
        far_in[...] = jnp.zeros_like(far_in)

    @pl.when(jnp.logical_not(has_far))
    def _():
        far_grad[...] = jnp.zeros_like(far_grad)

    def far_copy(column, step):
        at = rows(step)
        return pltpu.make_async_remote_copy(
            far_out.at[column, at], far_in.at[column, at],
            far_sems.at[0, column, step], far_sems.at[1, column, step],
            device_id=far_device,
        )

    def near_copy(column, step):
        at = rows(step)
        return pltpu.make_async_remote_copy(
            near_out.at[column, at], near_in.at[column, at],
            near_sems.at[0, column, step], near_sems.at[1, column, step],
            device_id=partner,
        )

    def across_copy(column, split):
        at = rows(split, tile)
        return pltpu.make_async_remote_copy(
            hidden_grad.at[column, at], near_grad.at[column, at],
            across_sems.at[0, column, split], across_sems.at[1, column, split],
            device_id=partner,
        )

    def relay_copy(column, split):
        at = rows(split, tile)
        return pltpu.make_async_remote_copy(
            near_grad.at[column, at], far_grad.at[column, at],
            relay_sems.at[0, column, split], relay_sems.at[1, column, split],
            device_id=back_device,
        )

    def gain():
        return norm_gain[...].reshape(1, channels)

    def normalized(at):
        signal_f = signal[at, :].astype(f32)
        mean_square = jnp.mean(signal_f * signal_f, axis=-1, keepdims=True)
        inverse_rms = lax.rsqrt(mean_square + epsilon)
        return signal_f, inverse_rms, signal_f * inverse_rms * gain()

    def side_of(column):
        return slice(column * block, (column + 1) * block)

    def activate(step):
        at = rows(step)
        _, _, normed = normalized(at)
        activated[at, :] = (normed * gelu_cdf(normed)).astype(bf16)

    def multiply_far(step):
        at = rows(step)
        result = dot(activated[at, :], conv_weight[far_tap], ((1,), (0,))).astype(bf16)
        for column in range(blocks):
            far_out[column, at, :] = result[:, side_of(column)]
        pl.when(has_far)(far_copy(0, step).start)

    def multiply(step):
        at = rows(step)
        value = activated[at, :]
        near_term[at, :] = dot(value, conv_weight[near_tap], ((1,), (0,)))
        hidden[at, :] = dot(value, conv_weight[1], ((1,), (0,)))
        gated_grad[at, :] = dot(cotangent[at, :], output_weight[...], ((1,), (1,)))
        transposed[:, at] = value.T
        cotangent_t[:, at] = cotangent[at, :].T

    def pass_near(column, step):
        at = rows(step)
        pl.when(has_back)(far_copy(column, step).wait_recv)
        near_out[column, at, :] = (
            near_term[at, side_of(column)] + far_in[column, at, :].astype(f32)
        ).astype(bf16)
        near_copy(column, step).start()

    def finish_hidden(column, step):
        at = rows(step)
        near_copy(column, step).wait_recv()
        value = hidden[at, side_of(column)] + near_in[column, at, :].astype(f32)
        cdf = gelu_cdf(value)
        hidden_grad[column, at, :] = (
            gated_grad[at, side_of(column)] * gelu_slope(value, cdf)
        ).astype(bf16)
        across_copy(column, step).start()
        gated[at, side_of(column)] = (value * cdf).astype(bf16)

    gain_load.wait()
    load_signal(0).wait()
    activate(0)
    conv_load.wait()
    pl.semaphore_wait(barrier, levels + 1)

    def produce(step, last, also=None):
        multiply_far(step)
        if also is not None:
            also()
        load_cotangent(step).wait()
        if not last:
            load_signal(step + 1).wait()
        multiply(step)
        if not last:
            activate(step + 1)

    produce(0, False, output_load.wait)

    @pl.loop(1, chunks - 1)
    def _(step):
        produce(step, False)
        pass_near(0, step - 1)

    produce(chunks - 1, True)
    pl.when(has_far)(far_copy(1, 0).start)

    def near(item, ahead=3):
        pass_near(*divmod(item, chunks))
        later = item + ahead
        if chunks <= later < blocks * chunks:
            pl.when(has_far)(far_copy(*divmod(later, chunks)).start)

    def turn(item):
        finish_hidden(*divmod(item, chunks))

    deep_units = (0, 1)
    slots = [(unit, 0, channels) for unit in range(2 * blocks)]
    if split_last:
        unit = slots.pop()[0]
        slots += [(unit, 0, half), (unit, half, half)]
    sent = [[] for _ in slots]


    def begin(slot, *copies):
        for copy in copies:
            copy.start()
            sent[slot].append(copy)

    def extent(slot):
        _, first, count = slots[slot]
        return pl.ds(first, count)

    def pair_copy(slot):
        unit, at = slots[slot][0], extent(slot)
        return pltpu.make_async_remote_copy(
            give.at[unit, at], from_sibling.at[unit, at],
            pair_sems.at[0, slot], pair_sems.at[1, slot],
            device_id=sibling,
        )

    def contribute(unit, multiply_tile):
        for slot, (other, first, count) in enumerate(slots):
            if other != unit:
                continue
            size = tile if count % tile == 0 else block

            @pl.loop(0, count // size)
            def _(step):
                at = pl.ds(pl.multiple_of(first + step * size, size), size)
                mine_part, their_part = multiply_tile(at)
                own[unit, at, :] = mine_part
                give[unit, at, :] = their_part.astype(bf16)

            begin(slot, pair_copy(slot))

    def contribute_first(unit):
        column = unit

        def multiply_tile(at):
            output_part = dot(cotangent_t[at, :], gated[:, side_of(column)], ((1,), (0,)))
            middle_part = dot(transposed[at, :], hidden_grad[column], ((1,), (0,)))
            return (
                jnp.where(core == 0, output_part, middle_part),
                jnp.where(core == 0, middle_part, output_part),
            )

        contribute(unit, multiply_tile)

    def contribute_second(unit):
        column = unit - blocks
        for split in range(splits):
            pl.when(has_far)(relay_copy(column, split).wait_recv)

        def multiply_tile(at):
            both = dot(
                transposed[at, :],
                jnp.concatenate([near_grad[column], far_grad[column]], axis=1),
                ((1,), (0,)),
            )
            near_part, far_part = both[:, :block], both[:, block:]
            return (
                jnp.where(core == odd, near_part, far_part),
                jnp.where(core == odd, far_part, near_part),
            )

        contribute(unit, multiply_tile)

    def landing(unit):
        return grads.at[unit // blocks, core, unit % blocks]

    distances = range(1, levels)
    my_layer = pl.ds(pl.multiple_of(depth * layer, layer), layer)
    my_thin = pl.ds(pl.multiple_of(depth * layer + odd * piece, piece), piece)
    their_thin = pl.ds(pl.multiple_of(depth * layer + (1 - odd) * piece, piece), piece)

    def deep_copy(unit, distance):
        other, device = level(distance)
        return pltpu.make_async_remote_copy(
            deep_send.at[unit, pl.ds(pl.multiple_of(other * layer, layer), layer)],
            deep_pieces.at[unit, distance - 1],
            z_sems.at[0, unit, distance - 1], z_sems.at[1, unit, distance - 1],
            device_id=device,
        )

    def thin_copy(unit):
        return pltpu.make_async_remote_copy(
            thin_send.at[unit], from_thin.at[unit], y_sems.at[0, unit], y_sems.at[1, unit],
            device_id=partner,
        )

    def thin_gather(unit):
        place = landing(unit).at[my_thin]
        return pltpu.make_async_remote_copy(
            place, place, yg_sems.at[0, unit], yg_sems.at[1, unit], device_id=partner,
        )

    def deep_gather(unit, distance):
        place = landing(unit).at[my_layer]
        return pltpu.make_async_remote_copy(
            place, place, zg_sems.at[0, unit, distance - 1], zg_sems.at[1, unit, distance - 1],
            device_id=level(distance)[1],
        )

    def whole_back(unit):
        place = landing(unit)
        return pltpu.make_async_remote_copy(
            place, place, back_sems.at[0, unit, 0], back_sems.at[1, unit, 0], device_id=sibling,
        )

    def deep(unit, stage):
        if stage == 1:
            pair_copy(unit).wait_recv()
            deep_send[unit] = (own[unit] + from_sibling[unit].astype(f32)).astype(bf16)
            begin(unit, *[deep_copy(unit, distance) for distance in distances])
        elif stage == 2:
            for distance in distances:
                deep_copy(unit, distance).wait_recv()
            for place in (their_thin, my_thin):
                total = own[unit, place, :] + from_sibling[unit, place, :].astype(f32)
                first = 0 if place is my_thin else 1
                within = pl.ds(
                    pl.multiple_of(piece * (odd if first == 0 else 1 - odd), piece), piece
                )
                for distance in distances:
                    total = total + deep_pieces[unit, distance - 1, within, :].astype(f32)
                if place is my_thin:
                    own[unit, place, :] = total
                else:
                    thin_send[unit] = total.astype(bf16)
                    begin(unit, thin_copy(unit))
        elif stage == 3:
            thin_copy(unit).wait_recv()
            total = own[unit, my_thin, :] + from_thin[unit].astype(f32)
            grads[unit // blocks, core, unit % blocks, my_thin, :] = total.astype(bf16)
            begin(unit, thin_gather(unit))
        elif stage == 4:
            thin_gather(unit).wait_recv()
            begin(unit, *[deep_gather(unit, distance) for distance in distances])
        elif stage == 5:
            for distance in distances:
                deep_gather(unit, distance).wait_recv()
            begin(unit, whole_back(unit))
        else:
            whole_back(unit).wait_recv()

    def flat(slot, stage):
        unit, first, count = slots[slot]
        middle, small = count // 2, count // 2 // levels

        def place(start, size):
            return pl.ds(pl.multiple_of(first + start, 16), size)

        mine, theirs = place(odd * middle, middle), place((1 - odd) * middle, middle)
        my_piece = place(odd * middle + depth * small, small)
        y_copy = pltpu.make_async_remote_copy(
            y_send.at[slot, pl.ds(0, middle)], from_y.at[slot, pl.ds(0, middle)],
            y_sems.at[0, slot], y_sems.at[1, slot],
            device_id=partner,
        )
        yg_copy = pltpu.make_async_remote_copy(
            landing(unit).at[mine], landing(unit).at[mine],
            yg_sems.at[0, slot], yg_sems.at[1, slot],
            device_id=partner,
        )

        def z_copy(distance):
            other, device = level(distance)
            return pltpu.make_async_remote_copy(
                z_send.at[slot, pl.ds(pl.multiple_of(other * small, small), small)],
                pieces.at[slot, distance - 1, pl.ds(0, small)],
                z_sems.at[0, slot, distance - 1], z_sems.at[1, slot, distance - 1],
                device_id=device,
            )

        def zg_copy(distance):
            return pltpu.make_async_remote_copy(
                landing(unit).at[my_piece], landing(unit).at[my_piece],
                zg_sems.at[0, slot, distance - 1], zg_sems.at[1, slot, distance - 1],
                device_id=level(distance)[1],
            )

        def back_copy(which):
            at = mine if which == 0 else theirs
            return pltpu.make_async_remote_copy(
                landing(unit).at[at], landing(unit).at[at],
                back_sems.at[0, slot, which], back_sems.at[1, slot, which],
                device_id=sibling,
            )

        if stage == 1:
            pair_copy(slot).wait_recv()
            y_send[slot, pl.ds(0, middle), :] = (
                own[unit, theirs, :] + from_sibling[unit, theirs, :].astype(f32)
            ).astype(bf16)
            begin(slot, y_copy)
        elif stage == 2:
            y_copy.wait_recv()
            total = (
                own[unit, mine, :]
                + from_sibling[unit, mine, :].astype(f32)
                + from_y[slot, pl.ds(0, middle), :].astype(f32)
            )
            own[unit, mine, :] = total
            z_send[slot, pl.ds(0, middle), :] = total.astype(bf16)
            begin(slot, *[z_copy(distance) for distance in distances])
        elif stage == 3:
            for distance in distances:
                z_copy(distance).wait_recv()
            total = own[unit, my_piece, :]
            for distance in distances:
                total = total + pieces[slot, distance - 1, pl.ds(0, small), :].astype(f32)
            grads[unit // blocks, core, unit % blocks, my_piece, :] = total.astype(bf16)
            begin(slot, *[zg_copy(distance) for distance in distances])
        elif stage == 4:
            for distance in distances:
                zg_copy(distance).wait_recv()
            begin(slot, yg_copy, back_copy(0))
        elif stage == 5:
            yg_copy.wait_recv()
            begin(slot, back_copy(1))
        else:
            back_copy(0).wait_recv()
            back_copy(1).wait_recv()

    def reduce(unit, stage):
        (deep if unit in deep_units else flat)(unit, stage)
        if stage == 6:
            for copy in sent[unit]:
                copy.wait_send()

    def relay(item):
        column, split = divmod(item, splits)
        across_copy(column, split).wait_recv()
        pl.when(has_back)(relay_copy(column, split).start)

    def write_out(step):
        at = rows(step, tile)
        block_out[at, :] = (
            signal[at, :].astype(f32) + dot(gated[at, :], output_weight[...], ((1,), (0,)))
        ).astype(bf16)

    def write_grad(step):
        at = rows(step, block)

        def joined(ref):
            return jnp.concatenate([ref[column, at, :] for column in range(blocks)], axis=1)

        signal_f, inverse_rms, normed = normalized(at)
        input_gradient = (
            dot(joined(hidden_grad), conv_weight[1], ((1,), (1,)))
            + dot(joined(near_grad), conv_weight[near_tap], ((1,), (1,)))
            + dot(joined(far_grad), conv_weight[far_tap], ((1,), (1,)))
        )
        weighted = input_gradient * gelu_slope(normed, gelu_cdf(normed)) * gain()
        inner = jnp.mean(weighted * signal_f, axis=-1, keepdims=True)
        cubed = inverse_rms * inverse_rms * inverse_rms
        signal_grad[at, :] = (
            cotangent[at, :].astype(f32) + weighted * inverse_rms - signal_f * cubed * inner
        ).astype(bf16)

    def write_grads(first, last):
        @pl.loop(first, last)
        def _(step):
            write_grad(step)

    def drain():
        for column in range(blocks):
            for split in range(splits):
                near_copy(column, split).wait_send()
                pl.when(has_far)(far_copy(column, split).wait_send)
                across_copy(column, split).wait_send()
                pl.when(has_back)(relay_copy(column, split).wait_send)

    turn(0)
    near(2)
    turn(1)
    near(3)
    near(4)
    relay(0)
    turn(2)
    relay(1)
    turn(3)
    contribute_first(0)
    turn(4)
    reduce(0, 1)
    near(5)
    near(6)
    near(7)
    relay(2)
    relay(3)
    relay(4)
    turn(5)
    turn(6)
    reduce(0, 2)
    turn(7)
    contribute_first(1)
    near(8)
    relay(5)
    near(9)
    reduce(1, 1)
    relay(6)
    near(10)
    reduce(0, 3)
    near(11)
    relay(7)
    turn(8)
    write_out(0)
    turn(9)
    write_out(1)
    turn(10)
    write_out(2)
    reduce(0, 4)
    turn(11)
    write_out(3)
    contribute_first(2)
    relay(8)
    contribute_second(4)
    relay(9)
    reduce(2, 1)
    relay(10)
    reduce(4, 1)
    reduce(0, 5)
    relay(11)
    contribute_second(3)
    reduce(0, 6)
    reduce(2, 2)
    reduce(3, 1)
    reduce(4, 2)
    contribute_second(5)
    write_grads(4, 6)
    reduce(2, 3)
    reduce(6, 1)
    reduce(3, 2)
    reduce(5, 1)
    write_grads(6, 8)
    reduce(4, 3)
    write_grads(0, 2)
    reduce(6, 2)
    write_grads(2, 4)
    reduce(5, 2)
    reduce(1, 2)
    reduce(2, 4)
    reduce(3, 3)
    reduce(1, 3)
    reduce(4, 4)
    reduce(6, 3)
    reduce(2, 5)
    reduce(5, 3)
    reduce(1, 4)
    reduce(2, 6)
    reduce(3, 4)
    reduce(4, 5)
    reduce(6, 4)
    reduce(4, 6)
    drain()
    reduce(5, 4)
    reduce(3, 5)
    reduce(6, 5)
    reduce(3, 6)
    reduce(6, 6)
    reduce(5, 5)
    reduce(1, 5)
    reduce(5, 6)
    reduce(1, 6)


def copy_results(
    grad_scale, block_out, signal_grad, grads, out0, out1, out2, out3, conv_grad, output_grad, sems
):
    blocks = grads.shape[2]
    block = grads.shape[4]
    copies = [
        pltpu.make_async_copy(block_out, out0, sems.at[0]),
        pltpu.make_async_copy(signal_grad, out1, sems.at[1]),
    ]
    for copy in copies:
        copy.start()
    for tap, (batch, owner) in enumerate(((1, 0), (0, 1), (1, 1))):
        for column in range(blocks):
            side = slice(column * block, (column + 1) * block)
            conv_grad[tap, :, side] = grads[batch, owner, column].astype(jnp.float32) * grad_scale
        copies.append(pltpu.make_async_copy(conv_grad.at[tap], out2.at[tap], sems.at[2 + tap]))
        copies[-1].start()
    for column in range(blocks):
        side = slice(column * block, (column + 1) * block)
        output_grad[side, :] = grads[0, 0, column].astype(jnp.float32).T * grad_scale
    copies.append(pltpu.make_async_copy(output_grad, out3, sems.at[5]))
    copies[-1].start()
    for copy in copies:
        copy.wait()


def run_whole_block(signal, norm_gain, conv_weight, output_weight, cotangent):
    devices = lax.axis_size("seq")
    levels = devices // 4
    bins, channels = signal.shape
    width = output_weight.shape[0]
    chunks = bins // 256
    blocks, block, splits = width // 128, 128, bins // 256
    units = 2 * blocks + 1
    bf16, f32 = jnp.bfloat16, jnp.float32
    vmem = pl.BlockSpec(memory_space=pltpu.VMEM)
    hbm = pl.BlockSpec(memory_space=pltpu.HBM)
    dma = pltpu.SemaphoreType.DMA
    narrow = pltpu.VMEM((bins, width), bf16)
    wide = pltpu.VMEM((bins, width), f32)
    stacked = pltpu.VMEM((blocks, bins, block), bf16)
    results = (
        jax.ShapeDtypeStruct((bins, channels), bf16),
        jax.ShapeDtypeStruct((bins, channels), bf16),
        jax.ShapeDtypeStruct((3, channels, width), f32),
        jax.ShapeDtypeStruct((width, channels), f32),
    )
    outs = pl.pallas_call(
        functools.partial(whole_block, devices, True),
        out_shape=(
            pltpu.VMEM((bins, channels), bf16),
            pltpu.VMEM((bins, channels), bf16),
            pltpu.VMEM((2, 2, blocks, channels, block), bf16),
        ),
        in_specs=[hbm] * 5,
        out_specs=(vmem,) * 3,
        scratch_shapes=[
            pltpu.VMEM((bins, channels), bf16),
            pltpu.VMEM((bins, channels), bf16),
            pltpu.VMEM((3, channels, width), bf16),
            pltpu.VMEM((width, channels), bf16),
            pltpu.VMEM((channels,), f32),
            pltpu.VMEM((bins, channels), bf16),
            pltpu.VMEM((channels, bins), bf16),
            pltpu.VMEM((channels, bins), bf16),
            wide, wide, wide, narrow,
            stacked, stacked, stacked, stacked,
            stacked, stacked, stacked,
            pltpu.VMEM((units, channels, block), f32),
            pltpu.VMEM((units, channels, block), bf16),
            pltpu.VMEM((units, channels, block), bf16),
            pltpu.VMEM((units, channels // 2, block), bf16),
            pltpu.VMEM((units, channels // 2, block), bf16),
            pltpu.VMEM((units, channels // 2, block), bf16),
            pltpu.VMEM((units, levels - 1, channels // 2 // levels, block), bf16),
            pltpu.VMEM((units, channels, block), bf16),
            pltpu.VMEM((units, levels - 1, channels // levels, block), bf16),
            pltpu.VMEM((units, channels // 2 // levels, block), bf16),
            pltpu.VMEM((units, channels // 2 // levels, block), bf16),
            dma((2 * chunks + 3,)),
            dma((2, blocks, splits)),
            dma((2, blocks, splits)),
            dma((2, blocks, splits)),
            dma((2, blocks, splits)),
            dma((2, units)),
            dma((2, units)),
            dma((2, units, levels - 1)),
            dma((2, units, levels - 1)),
            dma((2, units)),
            dma((2, units, 2)),
        ],
        compiler_params=pltpu.CompilerParams(
            collective_id=0, has_side_effects=True, vmem_limit_bytes=42 << 20
        ),
        name="whole_block",
    )(*[
        pltpu.with_memory_space_constraint(value, pltpu.HBM)
        for value in (signal, cotangent, conv_weight, output_weight, norm_gain)
    ])
    return pl.pallas_call(
        functools.partial(copy_results, 1.0 / math.sqrt(bins * devices)),
        out_shape=results,
        in_specs=[vmem] * 3,
        out_specs=(hbm,) * 4,
        scratch_shapes=[
            pltpu.VMEM((3, channels, width), f32), pltpu.VMEM((width, channels), f32), dma((6,))
        ],
        compiler_params=pltpu.CompilerParams(vmem_limit_bytes=16 << 20),
        name="copy_results",
    )(*outs)


def shards(signal, norm_gain, conv_weight, output_weight, cotangent):
    devices = lax.axis_size("seq")
    stride = devices // 8
    local_bins = signal.shape[0]
    if devices == 16:
        return run_whole_block(signal, norm_gain, conv_weight, output_weight, cotangent)
    odd = (lax.axis_index("seq") // stride) % 2 == 1
    far_weight = jnp.where(odd, conv_weight[0], conv_weight[2])
    near_weight = jnp.where(odd, conv_weight[2], conv_weight[0])
    far_route, near_route = [], []
    for i in range(devices):
        is_odd = (i // stride) % 2 == 1
        target = i + 2 * stride if is_odd else i - 2 * stride
        if 0 <= target < devices:
            far_route.append((i, target))
        near_route.append((i, i - stride if is_odd else i + stride))

    signal_f = signal.astype(jnp.float32)
    mean_square = jnp.mean(signal_f * signal_f, axis=-1, keepdims=True)
    inverse_rms = lax.rsqrt(mean_square + epsilon)
    normed = signal_f * inverse_rms * norm_gain
    normed_cdf = gelu_cdf(normed)
    activated = (normed * normed_cdf).astype(jnp.bfloat16)

    chunks = 2
    rows = local_bins // chunks
    parts = []
    for j in range(chunks):
        block = activated[j * rows : (j + 1) * rows]
        far = dot(block, far_weight, ((1,), (0,))).astype(jnp.bfloat16)
        parts.append(lax.ppermute(far, "seq", far_route))
    arrived = []
    for j in range(chunks):
        block = activated[j * rows : (j + 1) * rows]
        near = dot(block, near_weight, ((1,), (0,))) + parts[j].astype(jnp.float32)
        arrived.append(lax.ppermute(near.astype(jnp.bfloat16), "seq", near_route))
    hidden = dot(activated, conv_weight[1], ((1,), (0,))) + jnp.concatenate(arrived).astype(
        jnp.float32
    )
    hidden_cdf = gelu_cdf(hidden)
    gated = (hidden * hidden_cdf).astype(jnp.bfloat16)
    gated_grad = dot(cotangent, output_weight, ((1,), (1,)))
    hidden_grad = (gated_grad * gelu_slope(hidden, hidden_cdf)).astype(jnp.bfloat16)
    earlier = passed_along(hidden_grad, "seq", stride)
    later = passed_along(hidden_grad, "seq", -stride)

    grad_scale = 1.0 / math.sqrt(local_bins * devices)
    block_out = (signal_f + dot(gated, output_weight, ((1,), (0,)))).astype(jnp.bfloat16)
    output_term = dot(gated, cotangent, ((0,), (0,))) * grad_scale
    middle_term = dot(activated, hidden_grad, ((0,), (0,))) * grad_scale
    output_grad, middle_grad = lax.psum((output_term, middle_term), "seq")
    first_term = dot(activated, later, ((0,), (0,))) * grad_scale
    last_term = dot(activated, earlier, ((0,), (0,))) * grad_scale
    first_grad, last_grad = lax.psum((first_term, last_term), "seq")
    conv_grad = jnp.stack([first_grad, middle_grad, last_grad])

    input_gradient = (
        dot(hidden_grad, conv_weight[1], ((1,), (1,)))
        + dot(later, conv_weight[0], ((1,), (1,)))
        + dot(earlier, conv_weight[2], ((1,), (1,)))
    )
    weighted = input_gradient * gelu_slope(normed, normed_cdf) * norm_gain
    inner = jnp.mean(weighted * signal_f, axis=-1, keepdims=True)
    cubed = inverse_rms * inverse_rms * inverse_rms
    signal_grad = cotangent.astype(jnp.float32) + weighted * inverse_rms - signal_f * cubed * inner
    return (block_out, signal_grad.astype(jnp.bfloat16), conv_grad, output_grad)


def solution(mesh):
    placed = (P(("groups", "seq"), None), P(), P(), P(), P(("groups", "seq"), None))
    return jax.shard_map(
        shards,
        mesh=mesh,
        in_specs=placed,
        out_specs=(
            P(("groups", "seq"), None),
            P(("groups", "seq"), None),
            P("groups", None, None),
            P("groups", None),
        ),
        check_vma=False,
    )
```

```python
import functools
import math

import jax
import jax.numpy as jnp
from jax import lax
from jax.experimental import pallas as pl
from jax.experimental.pallas import tpu as pltpu
from jax.sharding import PartitionSpec as P

epsilon = 1e-06


def passed_along(block, axis, distance):
    devices = range(lax.axis_size(axis))
    route = [(i - distance, i) for i in devices if i - distance in devices]
    return lax.ppermute(block, axis, route)


def gelu_cdf(value):
    return 0.5 * (1.0 + jax.scipy.special.erf(value * (1.0 / math.sqrt(2.0))))


def gelu_slope(value, cdf):
    return cdf + value * jnp.exp(-0.5 * value * value) * (1.0 / math.sqrt(2.0 * math.pi))


def dot(left, right, contract):
    return lax.dot_general(left, right, (contract, ((), ())), preferred_element_type=jnp.float32)


def whole_block(
    devices, split_last, signal_hbm, cotangent_hbm, conv_hbm, output_hbm, gain_hbm,
    block_out, signal_grad, grads,
    signal, cotangent, conv_weight, output_weight, norm_gain,
    activated, transposed, cotangent_t, hidden, gated_grad, near_term, gated,
    far_out, far_in, near_out, near_in, hidden_grad, near_grad, far_grad,
    own, give, from_sibling, y_send, from_y, z_send, pieces,
    deep_send, deep_pieces, thin_send, from_thin,
    load_sems,
    far_sems, near_sems, across_sems, relay_sems,
    pair_sems, y_sems, z_sems, zg_sems, yg_sems, back_sems,
):
    channels, width = conv_weight.shape[1:]
    bins = signal.shape[0]
    bf16, f32 = jnp.bfloat16, jnp.float32
    me = lax.axis_index("seq")
    core, odd, depth = me % 2, (me // 2) % 2, me // 4
    levels = devices // 4
    sibling = {"seq": me + 1 - 2 * core}
    partner = {"seq": me + 2 - 4 * odd}
    far_tap, near_tap = 2 - 2 * odd, 2 * odd
    step_sign = 2 * odd - 1
    far_level, back_level = depth + step_sign, depth - step_sign
    has_far = jnp.logical_and(far_level >= 0, far_level < levels)
    has_back = jnp.logical_and(back_level >= 0, back_level < levels)
    far_device = {"seq": lax.rem(me + 4 * step_sign + devices, devices)}
    back_device = {"seq": lax.rem(me - 4 * step_sign + devices, devices)}
    chunk, tile, block = 256, 256, 128
    chunks = bins // chunk
    blocks = width // block
    half = channels // 2
    quarter, eighth = bins // 4, bins // 8
    whole_rows = [(i * quarter, quarter) for i in range(4)]
    first_rows = [(0, eighth), (eighth, eighth)] + whole_rows[1:]
    last_rows = whole_rows[:3] + [(bins - 2 * eighth, eighth), (bins - eighth, eighth)]
    items = [(0, *r) for r in first_rows]
    for column in range(1, blocks - 1):
        items += [(column, *r) for r in whole_rows]
    items += [(blocks - 1, *r) for r in last_rows]
    piece = half // levels
    layer = channels // levels

    def rows(step, size=chunk):
        if isinstance(step, int):
            return pl.ds(step * size, size)
        return pl.ds(pl.multiple_of(step * size, size), size)

    def level(distance):
        other = lax.rem(depth + distance, levels)
        return other, {"seq": other * 4 + odd * 2 + core}

    barrier = pltpu.get_barrier_semaphore()
    pl.semaphore_signal(barrier, inc=1, device_id=sibling)
    pl.semaphore_signal(barrier, inc=1, device_id=partner)
    for distance in range(1, levels):
        pl.semaphore_signal(barrier, inc=1, device_id=level(distance)[1])

    def load_signal(step):
        at = rows(step)
        return pltpu.make_async_copy(signal_hbm.at[at], signal.at[at], load_sems.at[step])

    def load_cotangent(step):
        at = rows(step)
        return pltpu.make_async_copy(
            cotangent_hbm.at[at], cotangent.at[at], load_sems.at[chunks + step]
        )

    conv_load = pltpu.make_async_copy(conv_hbm, conv_weight, load_sems.at[2 * chunks])
    output_load = pltpu.make_async_copy(output_hbm, output_weight, load_sems.at[2 * chunks + 1])
    gain_load = pltpu.make_async_copy(gain_hbm, norm_gain, load_sems.at[2 * chunks + 2])
    gain_load.start()
    load_signal(0).start()
    conv_load.start()
    output_load.start()
    load_cotangent(0).start()

    @pl.loop(1, chunks)
    def _(step):
        load_signal(step).start()
        load_cotangent(step).start()

    @pl.when(jnp.logical_not(has_back))
    def _():
        far_in[...] = jnp.zeros_like(far_in)

    @pl.when(jnp.logical_not(has_far))
    def _():
        far_grad[...] = jnp.zeros_like(far_grad)

    def far_copy(item):
        column, first, count = items[item]
        at = pl.ds(first, count)
        return pltpu.make_async_remote_copy(
            far_out.at[column, at], far_in.at[column, at],
            far_sems.at[0, item], far_sems.at[1, item],
            device_id=far_device,
        )

    def near_copy(item):
        column, first, count = items[item]
        at = pl.ds(first, count)
        return pltpu.make_async_remote_copy(
            near_out.at[column, at], near_in.at[column, at],
            near_sems.at[0, item], near_sems.at[1, item],
            device_id=partner,
        )

    def across_copy(item):
        column, first, count = items[item]
        at = pl.ds(first, count)
        return pltpu.make_async_remote_copy(
            hidden_grad.at[column, at], near_grad.at[column, at],
            across_sems.at[0, item], across_sems.at[1, item],
            device_id=partner,
        )

    def relay_copy(item):
        column, first, count = items[item]
        at = pl.ds(first, count)
        return pltpu.make_async_remote_copy(
            near_grad.at[column, at], far_grad.at[column, at],
            relay_sems.at[0, item], relay_sems.at[1, item],
            device_id=back_device,
        )

    def gain():
        return norm_gain[...].reshape(1, channels)

    def normalized(at):
        signal_f = signal[at, :].astype(f32)
        mean_square = jnp.mean(signal_f * signal_f, axis=-1, keepdims=True)
        inverse_rms = lax.rsqrt(mean_square + epsilon)
        return signal_f, inverse_rms, signal_f * inverse_rms * gain()

    def side_of(column):
        return slice(column * block, (column + 1) * block)

    def activate(at):
        _, _, normed = normalized(at)
        activated[at, :] = (normed * gelu_cdf(normed)).astype(bf16)

    def multiply_far(at):
        result = dot(activated[at, :], conv_weight[far_tap], ((1,), (0,))).astype(bf16)
        for column in range(blocks):
            far_out[column, at, :] = result[:, side_of(column)]

    def multiply_near(at):
        near_term[at, :] = dot(activated[at, :], conv_weight[near_tap], ((1,), (0,)))

    def multiply(at):
        value = activated[at, :]
        hidden[at, :] = dot(value, conv_weight[1], ((1,), (0,)))
        gated_grad[at, :] = dot(cotangent[at, :], output_weight[...], ((1,), (1,)))
        transposed[:, at] = value.T
        cotangent_t[:, at] = cotangent[at, :].T

    def send_far(item):
        pl.when(has_far)(far_copy(item).start)

    def near(item, ahead=3):
        column, first, count = items[item]
        at = pl.ds(first, count)
        pl.when(has_back)(far_copy(item).wait_recv)
        near_out[column, at, :] = (
            near_term[at, side_of(column)] + far_in[column, at, :].astype(f32)
        ).astype(bf16)
        near_copy(item).start()
        if len(first_rows) < item + ahead < len(items):
            send_far(item + ahead)

    def turn(item):
        column, first, count = items[item]
        at = pl.ds(first, count)
        near_copy(item).wait_recv()
        value = hidden[at, side_of(column)] + near_in[column, at, :].astype(f32)
        cdf = gelu_cdf(value)
        hidden_grad[column, at, :] = (
            gated_grad[at, side_of(column)] * gelu_slope(value, cdf)
        ).astype(bf16)
        across_copy(item).start()
        gated[at, side_of(column)] = (value * cdf).astype(bf16)

    def relay(item):
        across_copy(item).wait_recv()
        pl.when(has_back)(relay_copy(item).start)

    front, rest = pl.ds(0, eighth), pl.ds(eighth, eighth)
    step_rows = [pl.ds(first, count) for first, count in whole_rows]
    gain_load.wait()
    load_signal(0).wait()
    activate(front)
    conv_load.wait()
    multiply_far(front)
    pl.semaphore_wait(barrier, levels + 1)
    send_far(0)
    activate(rest)
    multiply_far(rest)
    send_far(1)
    multiply_near(step_rows[0])
    for step in range(1, 4):
        load_signal(step).wait()
        activate(step_rows[step])
        multiply_far(step_rows[step])
        send_far(step + 1)
        multiply_near(step_rows[step])
        if step < 3:
            near(step - 1)
    send_far(len(first_rows))
    output_load.wait()

    def multiply_rest(step):
        load_cotangent(step).wait()
        multiply(step_rows[step])

    deep_units = (0, 1)
    halving_units = (3,)
    slots = [(unit, 0, channels) for unit in range(2 * blocks)]
    if split_last:
        unit = slots.pop()[0]
        slots += [(unit, 0, half), (unit, half, half)]
    sent = [[] for _ in slots]


    def begin(slot, *copies):
        for copy in copies:
            copy.start()
            sent[slot].append(copy)

    def extent(slot):
        _, first, count = slots[slot]
        return pl.ds(first, count)

    def pair_copy(slot):
        unit, at = slots[slot][0], extent(slot)
        return pltpu.make_async_remote_copy(
            give.at[unit, at], from_sibling.at[unit, at],
            pair_sems.at[0, slot], pair_sems.at[1, slot],
            device_id=sibling,
        )

    def contribute(unit, multiply_tile):
        for slot, (other, first, count) in enumerate(slots):
            if other != unit:
                continue
            size = tile if count % tile == 0 else block

            @pl.loop(0, count // size)
            def _(step):
                at = pl.ds(pl.multiple_of(first + step * size, size), size)
                mine_part, their_part = multiply_tile(at)
                own[unit, at, :] = mine_part
                give[unit, at, :] = their_part.astype(bf16)

            begin(slot, pair_copy(slot))

    def contribute_first(unit):
        column = unit

        def multiply_tile(at):
            output_part = dot(cotangent_t[at, :], gated[:, side_of(column)], ((1,), (0,)))
            middle_part = dot(transposed[at, :], hidden_grad[column], ((1,), (0,)))
            return (
                jnp.where(core == 0, output_part, middle_part),
                jnp.where(core == 0, middle_part, output_part),
            )

        contribute(unit, multiply_tile)

    def contribute_second(unit):
        column = unit - blocks
        for item, (other, _, _) in enumerate(items):
            if other == column:
                pl.when(has_far)(relay_copy(item).wait_recv)

        def multiply_tile(at):
            both = dot(
                transposed[at, :],
                jnp.concatenate([near_grad[column], far_grad[column]], axis=1),
                ((1,), (0,)),
            )
            near_part, far_part = both[:, :block], both[:, block:]
            return (
                jnp.where(core == odd, near_part, far_part),
                jnp.where(core == odd, far_part, near_part),
            )

        contribute(unit, multiply_tile)

    def landing(unit):
        return grads.at[unit // blocks, core, unit % blocks]

    distances = range(1, levels)
    my_layer = pl.ds(pl.multiple_of(depth * layer, layer), layer)
    my_thin = pl.ds(pl.multiple_of(depth * layer + odd * piece, piece), piece)
    their_thin = pl.ds(pl.multiple_of(depth * layer + (1 - odd) * piece, piece), piece)

    def deep_copy(unit, distance):
        other, device = level(distance)
        return pltpu.make_async_remote_copy(
            deep_send.at[unit, pl.ds(pl.multiple_of(other * layer, layer), layer)],
            deep_pieces.at[unit, distance - 1],
            z_sems.at[0, unit, distance - 1], z_sems.at[1, unit, distance - 1],
            device_id=device,
        )

    def thin_copy(unit):
        return pltpu.make_async_remote_copy(
            thin_send.at[unit], from_thin.at[unit], y_sems.at[0, unit], y_sems.at[1, unit],
            device_id=partner,
        )

    def thin_gather(unit):
        place = landing(unit).at[my_thin]
        return pltpu.make_async_remote_copy(
            place, place, yg_sems.at[0, unit], yg_sems.at[1, unit], device_id=partner,
        )

    def deep_gather(unit, distance):
        place = landing(unit).at[my_layer]
        return pltpu.make_async_remote_copy(
            place, place, zg_sems.at[0, unit, distance - 1], zg_sems.at[1, unit, distance - 1],
            device_id=level(distance)[1],
        )

    def whole_back(unit):
        place = landing(unit)
        return pltpu.make_async_remote_copy(
            place, place, back_sems.at[0, unit, 0], back_sems.at[1, unit, 0], device_id=sibling,
        )

    def deep(unit, stage):
        if stage == 1:
            pair_copy(unit).wait_recv()
            deep_send[unit] = (own[unit] + from_sibling[unit].astype(f32)).astype(bf16)
            begin(unit, *[deep_copy(unit, distance) for distance in distances])
        elif stage == 2:
            for distance in distances:
                deep_copy(unit, distance).wait_recv()
            for place in (their_thin, my_thin):
                total = own[unit, place, :] + from_sibling[unit, place, :].astype(f32)
                first = 0 if place is my_thin else 1
                within = pl.ds(
                    pl.multiple_of(piece * (odd if first == 0 else 1 - odd), piece), piece
                )
                for distance in distances:
                    total = total + deep_pieces[unit, distance - 1, within, :].astype(f32)
                if place is my_thin:
                    own[unit, place, :] = total
                else:
                    thin_send[unit] = total.astype(bf16)
                    begin(unit, thin_copy(unit))
        elif stage == 3:
            thin_copy(unit).wait_recv()
            total = own[unit, my_thin, :] + from_thin[unit].astype(f32)
            grads[unit // blocks, core, unit % blocks, my_thin, :] = total.astype(bf16)
            begin(unit, thin_gather(unit))
        elif stage == 4:
            thin_gather(unit).wait_recv()
            begin(unit, *[deep_gather(unit, distance) for distance in distances])
        elif stage == 5:
            for distance in distances:
                deep_gather(unit, distance).wait_recv()
            begin(unit, whole_back(unit))
        else:
            whole_back(unit).wait_recv()

    def flat(slot, stage):
        unit, first, count = slots[slot]
        middle, small = count // 2, count // 2 // levels

        def place(start, size):
            return pl.ds(pl.multiple_of(first + start, 16), size)

        mine, theirs = place(odd * middle, middle), place((1 - odd) * middle, middle)
        my_piece = place(odd * middle + depth * small, small)
        y_copy = pltpu.make_async_remote_copy(
            y_send.at[slot, pl.ds(0, middle)], from_y.at[slot, pl.ds(0, middle)],
            y_sems.at[0, slot], y_sems.at[1, slot],
            device_id=partner,
        )
        yg_copy = pltpu.make_async_remote_copy(
            landing(unit).at[mine], landing(unit).at[mine],
            yg_sems.at[0, slot], yg_sems.at[1, slot],
            device_id=partner,
        )

        def z_copy(distance):
            other, device = level(distance)
            return pltpu.make_async_remote_copy(
                z_send.at[slot, pl.ds(pl.multiple_of(other * small, small), small)],
                pieces.at[slot, distance - 1, pl.ds(0, small)],
                z_sems.at[0, slot, distance - 1], z_sems.at[1, slot, distance - 1],
                device_id=device,
            )

        def zg_copy(distance):
            return pltpu.make_async_remote_copy(
                landing(unit).at[my_piece], landing(unit).at[my_piece],
                zg_sems.at[0, slot, distance - 1], zg_sems.at[1, slot, distance - 1],
                device_id=level(distance)[1],
            )

        def back_copy(which):
            at = mine if which == 0 else theirs
            return pltpu.make_async_remote_copy(
                landing(unit).at[at], landing(unit).at[at],
                back_sems.at[0, slot, which], back_sems.at[1, slot, which],
                device_id=sibling,
            )

        if stage == 1:
            pair_copy(slot).wait_recv()
            y_send[slot, pl.ds(0, middle), :] = (
                own[unit, theirs, :] + from_sibling[unit, theirs, :].astype(f32)
            ).astype(bf16)
            begin(slot, y_copy)
        elif stage == 2:
            y_copy.wait_recv()
            total = (
                own[unit, mine, :]
                + from_sibling[unit, mine, :].astype(f32)
                + from_y[slot, pl.ds(0, middle), :].astype(f32)
            )
            own[unit, mine, :] = total
            z_send[slot, pl.ds(0, middle), :] = total.astype(bf16)
            begin(slot, *[z_copy(distance) for distance in distances])
        elif stage == 3:
            for distance in distances:
                z_copy(distance).wait_recv()
            total = own[unit, my_piece, :]
            for distance in distances:
                total = total + pieces[slot, distance - 1, pl.ds(0, small), :].astype(f32)
            grads[unit // blocks, core, unit % blocks, my_piece, :] = total.astype(bf16)
            begin(slot, *[zg_copy(distance) for distance in distances])
        elif stage == 4:
            for distance in distances:
                zg_copy(distance).wait_recv()
            begin(slot, yg_copy, back_copy(0))
        elif stage == 5:
            yg_copy.wait_recv()
            begin(slot, back_copy(1))
        else:
            back_copy(0).wait_recv()
            back_copy(1).wait_recv()

    def halving(slot, stage):
        unit, first, count = slots[slot]
        middle = count // 2
        pairs, small = middle // 2, middle // 4
        low, high = depth % 2, depth // 2

        def place(start, size):
            return pl.ds(pl.multiple_of(first + start, 16), size)

        mine, theirs = place(odd * middle, middle), place((1 - odd) * middle, middle)
        keep = odd * middle + low * pairs
        my_pair = place(keep, pairs)
        my_piece = place(keep + high * small, small)
        beside = {"seq": me + 4 - 8 * low}
        across = {"seq": me + 8 - 16 * high}

        def remote(source, target, sems, where, device):
            return pltpu.make_async_remote_copy(
                source, target, sems.at[(0, *where)], sems.at[(1, *where)], device_id=device
            )

        def same(at, sems, where, device):
            return remote(landing(unit).at[at], landing(unit).at[at], sems, where, device)

        if stage in (1, 2):
            y_copy = remote(
                y_send.at[slot, pl.ds(0, middle)], from_y.at[slot, pl.ds(0, middle)],
                y_sems, (slot,), partner,
            )
        if stage in (2, 3):
            pair_send = remote(
                z_send.at[slot, pl.ds(0, pairs)], z_send.at[slot, pl.ds(pairs, pairs)],
                z_sems, (slot, 0), beside,
            )
        if stage in (3, 4):
            piece_send = remote(
                pieces.at[slot, 0, pl.ds(0, small)], pieces.at[slot, 1, pl.ds(0, small)],
                z_sems, (slot, 1), across,
            )
        if stage in (4, 5):
            piece_back = same(my_piece, zg_sems, (slot, 0), across)
        if stage in (5, 6):
            pair_back = same(my_pair, zg_sems, (slot, 1), beside)
        if stage in (6, 7):
            y_back = same(mine, yg_sems, (slot,), partner)
        if stage in (6, 8):
            first_back = same(mine, back_sems, (slot, 0), sibling)
        if stage in (7, 8):
            last_back = same(theirs, back_sems, (slot, 1), sibling)

        if stage == 1:
            pair_copy(slot).wait_recv()
            y_send[slot, pl.ds(0, middle), :] = (
                own[unit, theirs, :] + from_sibling[unit, theirs, :].astype(f32)
            ).astype(bf16)
            begin(slot, y_copy)
        elif stage == 2:
            y_copy.wait_recv()
            own[unit, mine, :] = (
                own[unit, mine, :]
                + from_sibling[unit, mine, :].astype(f32)
                + from_y[slot, pl.ds(0, middle), :].astype(f32)
            )
            z_send[slot, pl.ds(0, pairs), :] = own[
                unit, place(odd * middle + (1 - low) * pairs, pairs), :
            ].astype(bf16)
            begin(slot, pair_send)
        elif stage == 3:
            pair_send.wait_recv()
            own[unit, my_pair, :] = (
                own[unit, my_pair, :] + z_send[slot, pl.ds(pairs, pairs), :].astype(f32)
            )
            pieces[slot, 0, pl.ds(0, small), :] = own[
                unit, place(keep + (1 - high) * small, small), :
            ].astype(bf16)
            begin(slot, piece_send)
        elif stage == 4:
            piece_send.wait_recv()
            total = own[unit, my_piece, :] + pieces[slot, 1, pl.ds(0, small), :].astype(f32)
            grads[unit // blocks, core, unit % blocks, my_piece, :] = total.astype(bf16)
            begin(slot, piece_back)
        elif stage == 5:
            piece_back.wait_recv()
            begin(slot, pair_back)
        elif stage == 6:
            pair_back.wait_recv()
            begin(slot, y_back, first_back)
        elif stage == 7:
            y_back.wait_recv()
            begin(slot, last_back)
        else:
            first_back.wait_recv()
            last_back.wait_recv()

    def reduce(unit, stage):
        way = deep if unit in deep_units else halving if unit in halving_units else flat
        way(unit, stage)
        if stage == (8 if way is halving else 6):
            for copy in sent[unit]:
                copy.wait_send()

    def write_out(step):
        at = rows(step, tile)
        block_out[at, :] = (
            signal[at, :].astype(f32) + dot(gated[at, :], output_weight[...], ((1,), (0,)))
        ).astype(bf16)

    def write_grad(step):
        at = rows(step, block)

        def joined(ref):
            return jnp.concatenate([ref[column, at, :] for column in range(blocks)], axis=1)

        signal_f, inverse_rms, normed = normalized(at)
        input_gradient = (
            dot(joined(hidden_grad), conv_weight[1], ((1,), (1,)))
            + dot(joined(near_grad), conv_weight[near_tap], ((1,), (1,)))
            + dot(joined(far_grad), conv_weight[far_tap], ((1,), (1,)))
        )
        weighted = input_gradient * gelu_slope(normed, gelu_cdf(normed)) * gain()
        inner = jnp.mean(weighted * signal_f, axis=-1, keepdims=True)
        cubed = inverse_rms * inverse_rms * inverse_rms
        signal_grad[at, :] = (
            cotangent[at, :].astype(f32) + weighted * inverse_rms - signal_f * cubed * inner
        ).astype(bf16)

    def write_grads(first, last):
        @pl.loop(first, last)
        def _(step):
            write_grad(step)

    def drain():
        for item in range(len(items)):
            near_copy(item).wait_send()
            pl.when(has_far)(far_copy(item).wait_send)
            across_copy(item).wait_send()
            pl.when(has_back)(relay_copy(item).wait_send)

    near(2)
    multiply_rest(0)
    turn(0)
    turn(1)
    multiply_rest(1)
    near(3)
    near(4)
    multiply_rest(2)
    near(5)
    turn(2)
    relay(0)
    turn(3)
    multiply_rest(3)
    relay(1)
    turn(4)
    contribute_first(0)
    near(6)
    reduce(0, 1)
    relay(2)
    near(7)
    near(8)
    relay(3)
    turn(5)
    relay(4)
    near(9)
    turn(6)
    reduce(0, 2)
    turn(7)
    turn(8)
    contribute_first(1)
    relay(5)
    near(10)
    reduce(1, 1)
    reduce(0, 3)
    near(11)
    relay(6)
    near(12)
    contribute_second(3)
    relay(7)
    near(13)
    reduce(3, 1)
    relay(8)
    turn(9)
    turn(10)
    reduce(0, 4)
    turn(11)
    turn(12)
    reduce(1, 2)
    turn(13)
    reduce(3, 2)
    contribute_first(2)
    relay(9)
    relay(10)
    reduce(0, 5)
    reduce(3, 3)
    write_out(0)
    reduce(2, 1)
    contribute_second(4)
    relay(11)
    relay(12)
    reduce(4, 1)
    write_out(1)
    relay(13)
    write_out(2)
    reduce(0, 6)
    reduce(3, 4)
    reduce(1, 3)
    reduce(2, 2)
    contribute_second(5)
    reduce(4, 2)
    reduce(5, 1)
    reduce(3, 5)
    reduce(6, 1)
    reduce(2, 3)
    write_grads(3, 4)
    reduce(5, 2)
    reduce(3, 6)
    reduce(6, 2)
    write_grads(0, 1)
    reduce(4, 3)
    reduce(2, 4)
    write_out(3)
    write_grads(4, 5)
    reduce(3, 7)
    reduce(6, 3)
    write_grads(2, 3)
    reduce(5, 3)
    write_grads(1, 2)
    reduce(3, 8)
    reduce(1, 4)
    reduce(4, 4)
    write_grads(6, 7)
    reduce(6, 4)
    reduce(2, 5)
    write_grads(5, 6)
    drain()
    reduce(5, 4)
    reduce(4, 5)
    reduce(2, 6)
    reduce(6, 5)
    write_grads(7, 8)
    reduce(5, 5)
    reduce(6, 6)
    reduce(1, 5)
    reduce(5, 6)
    reduce(4, 6)
    reduce(1, 6)


def copy_results(
    grad_scale, block_out, signal_grad, grads, out0, out1, out2, out3, conv_grad, output_grad, sems
):
    blocks = grads.shape[2]
    block = grads.shape[4]
    copies = [
        pltpu.make_async_copy(block_out, out0, sems.at[0]),
        pltpu.make_async_copy(signal_grad, out1, sems.at[1]),
    ]
    for copy in copies:
        copy.start()
    for tap, (batch, owner) in enumerate(((1, 0), (0, 1), (1, 1))):
        for column in range(blocks):
            side = slice(column * block, (column + 1) * block)
            conv_grad[tap, :, side] = grads[batch, owner, column].astype(jnp.float32) * grad_scale
        copies.append(pltpu.make_async_copy(conv_grad.at[tap], out2.at[tap], sems.at[2 + tap]))
        copies[-1].start()
    for column in range(blocks):
        side = slice(column * block, (column + 1) * block)
        output_grad[side, :] = grads[0, 0, column].astype(jnp.float32).T * grad_scale
    copies.append(pltpu.make_async_copy(output_grad, out3, sems.at[5]))
    copies[-1].start()
    for copy in copies:
        copy.wait()


def run_whole_block(signal, norm_gain, conv_weight, output_weight, cotangent):
    devices = lax.axis_size("seq")
    levels = devices // 4
    bins, channels = signal.shape
    width = output_weight.shape[0]
    chunks = bins // 256
    blocks, block, splits = width // 128, 128, bins // 256
    units = 2 * blocks + 1
    bf16, f32 = jnp.bfloat16, jnp.float32
    vmem = pl.BlockSpec(memory_space=pltpu.VMEM)
    hbm = pl.BlockSpec(memory_space=pltpu.HBM)
    dma = pltpu.SemaphoreType.DMA
    narrow = pltpu.VMEM((bins, width), bf16)
    wide = pltpu.VMEM((bins, width), f32)
    stacked = pltpu.VMEM((blocks, bins, block), bf16)
    results = (
        jax.ShapeDtypeStruct((bins, channels), bf16),
        jax.ShapeDtypeStruct((bins, channels), bf16),
        jax.ShapeDtypeStruct((3, channels, width), f32),
        jax.ShapeDtypeStruct((width, channels), f32),
    )
    outs = pl.pallas_call(
        functools.partial(whole_block, devices, True),
        out_shape=(
            pltpu.VMEM((bins, channels), bf16),
            pltpu.VMEM((bins, channels), bf16),
            pltpu.VMEM((2, 2, blocks, channels, block), bf16),
        ),
        in_specs=[hbm] * 5,
        out_specs=(vmem,) * 3,
        scratch_shapes=[
            pltpu.VMEM((bins, channels), bf16),
            pltpu.VMEM((bins, channels), bf16),
            pltpu.VMEM((3, channels, width), bf16),
            pltpu.VMEM((width, channels), bf16),
            pltpu.VMEM((channels,), f32),
            pltpu.VMEM((bins, channels), bf16),
            pltpu.VMEM((channels, bins), bf16),
            pltpu.VMEM((channels, bins), bf16),
            wide, wide, wide, narrow,
            stacked, stacked, stacked, stacked,
            stacked, stacked, stacked,
            pltpu.VMEM((units, channels, block), f32),
            pltpu.VMEM((units, channels, block), bf16),
            pltpu.VMEM((units, channels, block), bf16),
            pltpu.VMEM((units, channels // 2, block), bf16),
            pltpu.VMEM((units, channels // 2, block), bf16),
            pltpu.VMEM((units, channels // 2, block), bf16),
            pltpu.VMEM((units, levels - 1, channels // 2 // levels, block), bf16),
            pltpu.VMEM((units, channels, block), bf16),
            pltpu.VMEM((units, levels - 1, channels // levels, block), bf16),
            pltpu.VMEM((units, channels // 2 // levels, block), bf16),
            pltpu.VMEM((units, channels // 2 // levels, block), bf16),
            dma((2 * chunks + 3,)),
            dma((2, 4 * blocks + 2)),
            dma((2, 4 * blocks + 2)),
            dma((2, 4 * blocks + 2)),
            dma((2, 4 * blocks + 2)),
            dma((2, units)),
            dma((2, units)),
            dma((2, units, levels - 1)),
            dma((2, units, levels - 1)),
            dma((2, units)),
            dma((2, units, 2)),
        ],
        compiler_params=pltpu.CompilerParams(
            collective_id=0, has_side_effects=True, vmem_limit_bytes=42 << 20
        ),
        name="whole_block",
    )(*[
        pltpu.with_memory_space_constraint(value, pltpu.HBM)
        for value in (signal, cotangent, conv_weight, output_weight, norm_gain)
    ])
    return pl.pallas_call(
        functools.partial(copy_results, 1.0 / math.sqrt(bins * devices)),
        out_shape=results,
        in_specs=[vmem] * 3,
        out_specs=(hbm,) * 4,
        scratch_shapes=[
            pltpu.VMEM((3, channels, width), f32), pltpu.VMEM((width, channels), f32), dma((6,))
        ],
        compiler_params=pltpu.CompilerParams(vmem_limit_bytes=16 << 20),
        name="copy_results",
    )(*outs)


def shards(signal, norm_gain, conv_weight, output_weight, cotangent):
    devices = lax.axis_size("seq")
    stride = devices // 8
    local_bins = signal.shape[0]
    if devices == 16:
        return run_whole_block(signal, norm_gain, conv_weight, output_weight, cotangent)
    odd = (lax.axis_index("seq") // stride) % 2 == 1
    far_weight = jnp.where(odd, conv_weight[0], conv_weight[2])
    near_weight = jnp.where(odd, conv_weight[2], conv_weight[0])
    far_route, near_route = [], []
    for i in range(devices):
        is_odd = (i // stride) % 2 == 1
        target = i + 2 * stride if is_odd else i - 2 * stride
        if 0 <= target < devices:
            far_route.append((i, target))
        near_route.append((i, i - stride if is_odd else i + stride))

    signal_f = signal.astype(jnp.float32)
    mean_square = jnp.mean(signal_f * signal_f, axis=-1, keepdims=True)
    inverse_rms = lax.rsqrt(mean_square + epsilon)
    normed = signal_f * inverse_rms * norm_gain
    normed_cdf = gelu_cdf(normed)
    activated = (normed * normed_cdf).astype(jnp.bfloat16)

    chunks = 2
    rows = local_bins // chunks
    parts = []
    for j in range(chunks):
        block = activated[j * rows : (j + 1) * rows]
        far = dot(block, far_weight, ((1,), (0,))).astype(jnp.bfloat16)
        parts.append(lax.ppermute(far, "seq", far_route))
    arrived = []
    for j in range(chunks):
        block = activated[j * rows : (j + 1) * rows]
        near = dot(block, near_weight, ((1,), (0,))) + parts[j].astype(jnp.float32)
        arrived.append(lax.ppermute(near.astype(jnp.bfloat16), "seq", near_route))
    hidden = dot(activated, conv_weight[1], ((1,), (0,))) + jnp.concatenate(arrived).astype(
        jnp.float32
    )
    hidden_cdf = gelu_cdf(hidden)
    gated = (hidden * hidden_cdf).astype(jnp.bfloat16)
    gated_grad = dot(cotangent, output_weight, ((1,), (1,)))
    hidden_grad = (gated_grad * gelu_slope(hidden, hidden_cdf)).astype(jnp.bfloat16)
    earlier = passed_along(hidden_grad, "seq", stride)
    later = passed_along(hidden_grad, "seq", -stride)

    grad_scale = 1.0 / math.sqrt(local_bins * devices)
    block_out = (signal_f + dot(gated, output_weight, ((1,), (0,)))).astype(jnp.bfloat16)
    output_term = dot(gated, cotangent, ((0,), (0,))) * grad_scale
    middle_term = dot(activated, hidden_grad, ((0,), (0,))) * grad_scale
    output_grad, middle_grad = lax.psum((output_term, middle_term), "seq")
    first_term = dot(activated, later, ((0,), (0,))) * grad_scale
    last_term = dot(activated, earlier, ((0,), (0,))) * grad_scale
    first_grad, last_grad = lax.psum((first_term, last_term), "seq")
    conv_grad = jnp.stack([first_grad, middle_grad, last_grad])

    input_gradient = (
        dot(hidden_grad, conv_weight[1], ((1,), (1,)))
        + dot(later, conv_weight[0], ((1,), (1,)))
        + dot(earlier, conv_weight[2], ((1,), (1,)))
    )
    weighted = input_gradient * gelu_slope(normed, normed_cdf) * norm_gain
    inner = jnp.mean(weighted * signal_f, axis=-1, keepdims=True)
    cubed = inverse_rms * inverse_rms * inverse_rms
    signal_grad = cotangent.astype(jnp.float32) + weighted * inverse_rms - signal_f * cubed * inner
    return (block_out, signal_grad.astype(jnp.bfloat16), conv_grad, output_grad)


def solution(mesh):
    placed = (P(("groups", "seq"), None), P(), P(), P(), P(("groups", "seq"), None))
    return jax.shard_map(
        shards,
        mesh=mesh,
        in_specs=placed,
        out_specs=(
            P(("groups", "seq"), None),
            P(("groups", "seq"), None),
            P("groups", None, None),
            P("groups", None),
        ),
        check_vma=False,
    )
```
